256 devices in a mesh: dp: 4 (over y), ctx: 4 (over x), exp: 16 (over z, core).
Axes of the slice: x: 4, y: 4, z: 8, core: 2. Of those that a mesh axis runs over, the one named last changes fastest.
Arguments:
- residual: bfloat16 [4, 768, 4096], P('dp', 'ctx', 'exp'), may hold values from -80 to 80
- ssm_input: bfloat16 [4, 768, 4096], P('dp', 'ctx', 'exp'), may hold values from -80 to 80
- ssm_gate: bfloat16 [4, 768, 4096], P('dp', 'ctx', 'exp'), may hold values from -6 to 6
- input_map: bfloat16 [4, 768, 128], P('dp', 'ctx'), may hold values from -2 to 2
- output_map: bfloat16 [4, 768, 128], P('dp', 'ctx'), may hold values from -2 to 2
- step_raw: float32 [4, 768, 64], P('dp', 'ctx', 'exp'), may hold values from -2 to 2304
- log_rate: float32 [64], P('exp'), may hold values from -12 to 2
- skip_gain: float32 [64], P('exp'), may hold values from 0.5 to 1.5
- head_gain: float32 [4096], P('exp'), may hold values from 0.1 to 1.9
- moe_gain: float32 [4096], replicated, may hold values from 0.1 to 1.9
- expert_ids: int32 [4, 768, 2], P('dp', 'ctx'), may hold values from 0 to 15, all different within a row; in each aligned block of 12 rows (0 to 11, 12 to 23, ..., all dimensions but the last counted through in order) at most 4 rows name the same one
- gate_weight: float32 [4, 768, 2], P('dp', 'ctx'), may hold values from 0.1 to 1
- expert_up: bfloat16 [16, 4096, 12288], P('exp', None, ('dp', 'ctx')), may hold values from -0.09375 to 0.09375
- expert_down: bfloat16 [16, 12288, 4096], P('exp', ('dp', 'ctx')), may hold values from -0.0546875 to 0.0546875
Outputs:
- hidden: bfloat16 [4, 768, 4096], P('dp', 'ctx', 'exp')
- moe_out: bfloat16 [4, 768, 4096], P('dp', ('ctx', 'exp'))
The draws below stay inside these ranges and needn't reach their ends.
Inputs may be any that keep to these rules, and one draw needn't show every extreme that they name: `expert_ids`: within each aligned block of 12 positions of one sequence, no expert is named by more than 4 routes; some expert is named by exactly 4 routes in some block; the two routes of a position name different experts.
All inputs are finite; a program needn't handle non-finite values.
Results may differ from the reference program's by a relative error of at most 0.02.
Values may be sent and summed in bfloat16 or wider, within the bound.
A program may use at most 64 MiB of HBM per device.

```python
import math
import jax
import jax.numpy as jnp
import numpy as np
from jax import lax

HEADS = 64
HEADDIM = 64
STATE = 128
FFD = 768
TOKM = 12
D = 4096
FF = 12288
EXPERTS = 16
BATCH = 4
L_DEV = 192
SEQLEN = 768
CAP = 4
N_DP = 4
N_CTX = 4


def head_rates(key):
    mixed_key = jax.random.fold_in(key, 101)
    order_key, fast_key, slow_key = jax.random.split(mixed_key, 3)
    order = jax.random.permutation(order_key, HEADS)
    quick_channel_count = HEADS // 2
    quick = order < quick_channel_count
    fast_rate = jnp.exp(jax.random.uniform(fast_key, (HEADS,), jnp.float32, math.log(4.0), math.log(6.4))) / L_DEV
    slow_rate = jnp.exp(jax.random.uniform(slow_key, (HEADS,), jnp.float32, math.log(0.2), math.log(0.6))) / SEQLEN
    return (jnp.where(quick, fast_rate, slow_rate), quick)


def spike_mask(key):
    spots = jax.random.randint(jax.random.fold_in(key, 202), (BATCH, 2), 0, SEQLEN)
    positions = jnp.arange(SEQLEN)
    return jnp.any(positions[None, :, None] == spots[:, None, :], axis=2)


def draw_log_rate(key, part):
    rates, quick = head_rates(key)
    return jnp.log(rates)


def draw_step_raw(key, part):
    rates, quick = head_rates(key)
    token_markers = spike_mask(key)
    base_key, stretch_key, strength_key = jax.random.split(jax.random.fold_in(key, 303), 3)
    base = jnp.exp(jax.random.uniform(base_key, (BATCH, SEQLEN, HEADS), jnp.float32, math.log(0.5), 0.0))
    stretch_factor = jnp.exp(jax.random.uniform(stretch_key, (BATCH, SEQLEN // L_DEV, HEADS), jnp.float32, math.log(0.5), math.log(1.5)))
    steps = base * jnp.repeat(stretch_factor, L_DEV, axis=1)
    spike_strength = jnp.exp(jax.random.uniform(strength_key, (BATCH, SEQLEN, HEADS), jnp.float32, math.log(0.22), math.log(0.6)))
    bursting = token_markers[:, :, None] & jnp.logical_not(quick)[None, None, :]
    steps = jnp.where(bursting, spike_strength / rates[None, None, :], steps)
    return steps + jnp.log(-jnp.expm1(-steps))


def draw_ssm_input(key, part):
    rates, quick = head_rates(key)
    token_markers = spike_mask(key)
    noise_key = jax.random.fold_in(jax.random.fold_in(key, 404), 0)
    values = jax.random.normal(noise_key, (BATCH, SEQLEN, D), jnp.float32)
    slow_channel = jnp.repeat(jnp.logical_not(quick), HEADDIM)
    quiet = token_markers[:, :, None] & slow_channel[None, None, :]
    return jnp.where(quiet, 0.04 * values, values).astype(jnp.bfloat16)


def draw_residual(key, part):
    noise_key = jax.random.fold_in(jax.random.fold_in(key, 505), 0)
    values = jax.random.normal(noise_key, (BATCH, SEQLEN, D), jnp.float32)
    return values.astype(jnp.bfloat16)


def levels(rng, shape, shards, least, largest):
    def one(dim, parts):
        draws = jax.random.uniform(jax.random.fold_in(jax.random.fold_in(rng, 6), dim), (parts,), jnp.float32, least / len(shards), largest / len(shards))
        return jnp.repeat(jnp.exp(draws), shape[dim] // parts).reshape((-1,) + (1,) * (len(shape) - dim - 1))

    gain = one(*shards[0])
    for cut in shards[1:]:
        gain = gain * one(*cut)
    return gain


def assign_block(key, own, number, rows, number_of, top, bound, skew):
    order = jax.random.permutation(key, number_of)
    crowded, ordinary = shares(number_of, rows * top, bound, skew, True), shares(number_of, rows * top, bound, skew, False)
    places = jnp.arange(number_of)

    def named(lengths, offset_by):
        used = int((lengths > 0).sum())
        fixed = max(1, used // 4)
        moved = fixed + (places - fixed + offset_by * (used - fixed)) % max(1, number_of - fixed)
        return jnp.zeros((number_of,), jnp.int32).at[order[jnp.where(places < fixed, places, moved)]].set(jnp.asarray(lengths, jnp.int32))

    lengths = jnp.where(number % 4 == 0, named(crowded, number // 4), named(ordinary, number - number // 4 - 1))
    mixed = jax.random.permutation(jax.random.fold_in(own, 3), number_of)
    donor, sink = mixed[0:number_of // 2 * 2:2], mixed[1:number_of // 2 * 2:2]
    room = jnp.minimum(lengths[donor] - 1, bound - lengths[sink]) // 2
    room = jnp.where((donor == order[0]) | (sink == order[0]) | (lengths[sink] == 0), 0, jnp.maximum(room, 0))
    moved = jax.random.randint(jax.random.fold_in(own, 4), (number_of // 2,), 0, 1 << 20) % (room + 1)
    lengths = lengths.at[donor].add(-moved).at[sink].add(moved)
    labels = jnp.searchsorted(jnp.cumsum(lengths), jnp.arange(rows * top), side="right").astype(jnp.int32)
    listing = labels.reshape(top, rows).T
    listing = listing[jax.random.permutation(jax.random.fold_in(own, 1), rows)]
    offset_by = jax.random.randint(jax.random.fold_in(own, 2), (rows, 1), 0, top)
    return jnp.take_along_axis(listing, (jnp.arange(top)[None, :] + offset_by) % top, axis=1)


def shares(number_of, total, bound, skew, full):
    portions = [(1 << 20) // math.isqrt(standing ** skew) + 1 for standing in range(1, number_of + 1)]
    largest = bound if full else min(bound, max(-(-total // number_of), total * portions[0] // sum(portions)))
    least = 1 if total - largest >= number_of - 1 else 0
    given, surplus = [largest] + [least] * (number_of - 1), total - largest - least * (number_of - 1)
    while surplus > 0:
        movable = [i for i in range(1, number_of) if given[i] < largest] or [i for i in range(1, number_of) if given[i] < bound]
        mass, left = sum([portions[i] for i in movable]), surplus
        for i in movable:
            extra = min(bound - given[i], max(1, left * portions[i] // mass), surplus)
            given[i] = given[i] + extra
            surplus = surplus - extra
    return np.array(given)


def gaussian(rng, extent, scale, limit, cuts=(), held_as=jnp.bfloat16):
    array = jax.random.normal(rng, extent, jnp.float32) * scale
    if len(cuts) > 0:
        array = levels(rng, extent, cuts, -0.22, 0.18) * array
    return jnp.clip(array, min=-limit, max=limit).astype(held_as)


def setup_inputs(seed: int = 0) -> dict:
    seeds = jax.random.split(jax.random.key(seed), 15)
    residual = draw_residual(jax.random.fold_in(seeds[14], 71), 0)
    ssm_input = draw_ssm_input(jax.random.fold_in(seeds[14], 71), 0)
    ssm_gate = gaussian(seeds[2], (BATCH, SEQLEN, D), 1.0, 6.0, ((0, 4), (1, 4), (2, 16)))
    input_map = gaussian(seeds[3], (BATCH, SEQLEN, STATE), 0.3, 2.0, ((0, 4), (1, 4)))
    output_map = gaussian(seeds[4], (BATCH, SEQLEN, STATE), 0.3, 2.0, ((0, 4), (1, 4)))
    step_raw = draw_step_raw(jax.random.fold_in(seeds[14], 71), 0)
    log_rate = draw_log_rate(jax.random.fold_in(seeds[14], 71), 0)
    skip_gain = jnp.clip(0.5 + 1.0 * jax.random.uniform(seeds[7], (HEADS,), jnp.float32) ** levels(seeds[7], (HEADS,), ((0, 16),), -0.2, 0.2), 0.5, 1.5)
    head_gain = jnp.clip(1.0 + 0.18 * jax.random.normal(seeds[8], (D,), jnp.float32), 0.1, 1.9)
    moe_gain = jnp.clip(1.0 + 0.18 * jax.random.normal(seeds[9], (D,), jnp.float32), 0.1, 1.9)
    expert_ids_keys = jax.random.split(jax.random.fold_in(seeds[10], 1), BATCH * SEQLEN // TOKM)
    expert_ids_turns = jax.random.permutation(jax.random.fold_in(seeds[10], 3), BATCH * SEQLEN // TOKM)
    expert_ids = jax.vmap(lambda own, number: assign_block(jax.random.fold_in(seeds[10], 2), own, number, TOKM, EXPERTS, 2, CAP, 3))(expert_ids_keys, expert_ids_turns).reshape((BATCH, SEQLEN, 2))
    gate_weight = jnp.clip(0.1 + 0.9 * jax.random.uniform(seeds[11], (BATCH, SEQLEN, 2), jnp.float32) ** levels(seeds[11], (BATCH, SEQLEN, 2), ((0, 4), (1, 4)), -0.2, 0.2), 0.1, 1.0)
    expert_up = gaussian(seeds[12], (EXPERTS, D, FF), D ** -0.5, 0.09375, ((0, 16), (2, 16)))
    expert_down = gaussian(seeds[13], (EXPERTS, FF, D), FF ** -0.5, 0.0546875, ((0, 16), (1, 16)))
    return dict(residual=residual, ssm_input=ssm_input, ssm_gate=ssm_gate, input_map=input_map, output_map=output_map, step_raw=step_raw, log_rate=log_rate, skip_gain=skip_gain, head_gain=head_gain, moe_gain=moe_gain, expert_ids=expert_ids, gate_weight=gate_weight, expert_up=expert_up, expert_down=expert_down)


EPSILON = 1e-05

def route_slots(routes, experts):
    blocks = routes.shape[0]
    ordered = routes.reshape(blocks, -1)
    matches = (ordered[:, :, None] == jnp.arange(experts, dtype=jnp.int32)[None, None, :]).astype(jnp.int32)
    earlier = jnp.cumsum(matches, axis=1) - matches
    return lax.optimization_barrier(jnp.sum(earlier * matches, axis=2)).reshape(routes.shape).astype(jnp.int32)

def reference(residual, ssm_input, ssm_gate, input_map, output_map, step_raw, log_rate, skip_gain, head_gain, moe_gain, expert_ids, gate_weight, expert_up, expert_down):
    step_size = jax.nn.softplus(step_raw)
    cumulative = jnp.cumsum(step_size * (-jnp.exp(log_rate))[None, None, :], axis=1)
    values = ssm_input.astype(jnp.float32).reshape(BATCH, SEQLEN, HEADS, HEADDIM)
    positions = jnp.arange(SEQLEN)
    causal = positions[:, None] >= positions[None, :]

    def one_sequence(operands):
        cum_seq, in_map, out_map, steps_seq, values_seq = operands
        scores = jnp.dot(out_map, in_map.T, preferred_element_type=jnp.float32)

        def one_head(head_ops):
            cum_head, step_head, values_head = head_ops
            spread = cum_head[:, None] - cum_head[None, :]
            kernel = jnp.where(causal, jnp.exp(jnp.minimum(spread, 0.0)), 0.0) * scores * step_head[None, :]
            return jnp.dot(kernel, values_head, precision=lax.Precision.HIGHEST)
        return lax.map(one_head, (cum_seq.T, steps_seq.T, jnp.transpose(values_seq, (1, 0, 2))))
    per_head = lax.map(one_sequence, (cumulative, input_map, output_map, step_size, values))
    mixed_y = jnp.transpose(per_head, (0, 2, 1, 3)) + skip_gain[None, None, :, None] * values
    gates = jax.nn.silu(ssm_gate.astype(jnp.float32).reshape(BATCH, SEQLEN, HEADS, HEADDIM))
    gated = mixed_y * gates
    normed = gated * lax.rsqrt(lax.optimization_barrier(jnp.mean(gated * gated, axis=3, keepdims=True)) + EPSILON) * head_gain.reshape(HEADS, HEADDIM)
    hidden = (residual.astype(jnp.float32) + normed.reshape(BATCH, SEQLEN, D)).astype(jnp.bfloat16)
    hidden_wide = hidden.astype(jnp.float32)
    normal_rows = (hidden_wide * lax.rsqrt(lax.optimization_barrier(jnp.mean(hidden_wide * hidden_wide, axis=2, keepdims=True)) + EPSILON) * moe_gain[None, None, :]).astype(jnp.bfloat16)
    blocks = BATCH * SEQLEN // TOKM
    routes = expert_ids.reshape(blocks, TOKM, 2)
    slots = route_slots(routes, EXPERTS)
    block_ids = jnp.broadcast_to(jnp.arange(blocks, dtype=jnp.int32)[:, None, None], routes.shape)
    rows_in = jnp.broadcast_to(normal_rows.reshape(blocks, TOKM, 1, D), (blocks, TOKM, 2, D))
    buffer = jnp.zeros((EXPERTS, blocks, CAP, D), jnp.bfloat16).at[routes, block_ids, slots].set(rows_in)
    groups = N_DP * N_CTX

    def one_expert(operands):
        rows_expert, up_expert, down_expert = operands
        activated = jax.nn.silu(jnp.dot(rows_expert, up_expert, preferred_element_type=jnp.float32)).astype(jnp.bfloat16)
        row_count = activated.shape[0]
        act_groups = jnp.transpose(activated.reshape(row_count, groups, FFD), (1, 0, 2))
        down_groups = down_expert.reshape(groups, FFD, D)

        def add_group(total, group_operations):
            act_part, down_part = group_operations
            partial_sum = jnp.dot(act_part, down_part, preferred_element_type=jnp.float32).astype(jnp.bfloat16)
            partial_sum = lax.optimization_barrier(partial_sum)
            return (total + partial_sum.astype(jnp.float32), None)
        total, unused = lax.scan(add_group, jnp.zeros((row_count, D), jnp.float32), (act_groups, down_groups))
        return total.astype(jnp.bfloat16)
    outputs = lax.map(one_expert, (buffer.reshape(EXPERTS, blocks * CAP, D), expert_up, expert_down))
    outputs = outputs.reshape(EXPERTS, blocks, CAP, D)
    picked = outputs[routes, block_ids, slots].astype(jnp.float32)
    combined = lax.optimization_barrier(jnp.sum(gate_weight.reshape(blocks, TOKM, 2)[:, :, :, None] * picked, axis=2))
    moe_out = combined.astype(jnp.bfloat16).reshape(BATCH, SEQLEN, D)
    return (hidden, moe_out)
```

```python
import jax
import jax.numpy as jnp
from jax import lax
from jax.experimental import pallas as pl
from jax.experimental.pallas import tpu as pltpu
from jax.sharding import PartitionSpec as P

EPSILON = 1e-05


def shifted(block, axis, distance):
    devices = range(lax.axis_size(axis))
    route = [(i - distance, i) for i in devices if i - distance in devices]
    return lax.ppermute(block, axis, route)


def route_slots(routes, experts):
    blocks = routes.shape[0]
    ordered = routes.reshape(blocks, -1)
    matches = (ordered[:, :, None] == jnp.arange(experts, dtype=jnp.int32)[None, None, :]).astype(
        jnp.int32
    )
    earlier = jnp.cumsum(matches, axis=1) - matches
    return jnp.sum(earlier * matches, axis=2).reshape(routes.shape)


ROWS = 16
MESH = pl.DeviceIdType.MESH


def plane_kernel(
    x_ref, up_hbm, down_hbm, out_ref,
    gath, part, red1, red2, act, up_v, down_v,
    wsem, ag_send, ag_recv, r1_send, r1_recv, r2_send, r2_recv,
):
    dp, ctx, ex = lax.axis_index("dp"), lax.axis_index("ctx"), lax.axis_index("exp")
    n = 4
    width = x_ref.shape[1]
    ffd = up_v.shape[1]

    def rows(p, j):
        return pl.ds(pl.multiple_of((p * n + j) * ROWS, ROWS), ROWS)

    def target(p, phase):
        step = 1 - 2 * lax.rem(p, 2)
        on_ctx = lax.rem(p // 2 + phase, 2)
        d = lax.rem(dp + n + step * on_ctx, n)
        c = lax.rem(ctx + n + step * (1 - on_ctx), n)
        return (d, c, ex)

    def gather(s, p, j):
        if s == 0:
            src, phase = gath.at[0, rows(p, j - 1), :], 0
        else:
            src, phase = gath.at[s - 1, rows(p, j), :], 1
        return pltpu.make_async_remote_copy(
            src_ref=src, dst_ref=gath.at[s, rows(p, j), :],
            send_sem=ag_send.at[s, p, j], recv_sem=ag_recv.at[s, p, j],
            device_id=target(p, phase), device_id_type=MESH,
        )

    def first_gather(s, p, j, phase):
        return pltpu.make_async_remote_copy(
            src_ref=x_ref.at[pl.ds(pl.multiple_of(p * ROWS, ROWS), ROWS), :],
            dst_ref=gath.at[s, rows(p, j), :],
            send_sem=ag_send.at[s, p, j], recv_sem=ag_recv.at[s, p, j],
            device_id=target(p, phase), device_id_type=MESH,
        )

    def reduce1(s, p, j):
        return pltpu.make_async_remote_copy(
            src_ref=part.at[s, rows(p, j), :], dst_ref=red1.at[s - 1, rows(p, j), :],
            send_sem=r1_send.at[s - 1, p, j], recv_sem=r1_recv.at[s - 1, p, j],
            device_id=target(p, 1), device_id_type=MESH,
        )

    def reduce2(k, p):
        return pltpu.make_async_remote_copy(
            src_ref=part.at[0, rows(p, k), :], dst_ref=red2.at[k - 1, rows(0, p), :],
            send_sem=r2_send.at[k - 1, p], recv_sem=r2_recv.at[k - 1, p],
            device_id=target(p, 0), device_id_type=MESH,
        )

    up_copy = pltpu.make_async_copy(up_hbm, up_v, wsem.at[0])
    down_copy = pltpu.make_async_copy(down_hbm, down_v, wsem.at[1])
    up_copy.start()
    down_copy.start()

    barrier = pltpu.get_barrier_semaphore()
    for p in (0, 1, 2, 3):
        pl.semaphore_signal(barrier, inc=1, device_id=target(p, 0), device_id_type=MESH)
    pl.semaphore_wait(barrier, 4)

    @pl.loop(0, 4)
    def _(p):
        first_gather(0, p, 1, 0).start()
        first_gather(1, p, 0, 1).start()

    @pl.loop(0, 4)
    def _(p):
        gath[0, rows(p, 0), :] = x_ref[pl.ds(pl.multiple_of(p * ROWS, ROWS), ROWS), :]

    def forward(s, j):
        @pl.loop(0, 4)
        def _(p):
            gather(s, p, j).wait_recv()
            if s == 0 and j < 3:
                gather(0, p, j + 1).start()
            if s < 3:
                gather(s + 1, p, j).start()

    def up(s, c):
        cols = pl.ds(pl.multiple_of(c * 256, 256), 256)
        h = jnp.dot(gath[s], up_v[:, cols], preferred_element_type=jnp.float32)
        act[:, cols] = jax.nn.silu(h).astype(jnp.bfloat16)

    def down(s, c):
        cols = pl.ds(pl.multiple_of(c * 512, 512), 512)
        part[s, :, cols] = jnp.dot(
            act[...], down_v[:, cols], preferred_element_type=jnp.float32
        ).astype(jnp.bfloat16)

    def ups(s):
        @pl.loop(0, ffd // 256)
        def _(c):
            up(s, c)

    def downs(s, lo, hi):
        @pl.loop(lo, hi)
        def _(c):
            down(s, c)

    nd = width // 512

    def add(dst, d_idx, src, s_idx):
        dst[d_idx] = (
            dst[d_idx].astype(jnp.float32) + src[s_idx].astype(jnp.float32)
        ).astype(jnp.bfloat16)

    forward(0, 1)
    forward(0, 2)
    forward(1, 0)
    forward(0, 3)
    up_copy.wait()
    down_copy.wait()
    ups(0)
    forward(1, 1)
    downs(0, 0, nd // 2)
    forward(1, 2)
    downs(0, nd // 2, nd)
    forward(1, 3)
    forward(2, 0)
    ups(1)
    forward(2, 1)
    downs(1, 0, nd // 2)
    forward(2, 2)
    downs(1, nd // 2, nd)
    forward(2, 3)
    for j in (1, 2, 3, 0):
        @pl.loop(0, 4)
        def _(p):
            reduce1(1, p, j).start()
    ups(2)
    downs(2, 0, nd)
    for j in range(4):
        forward(3, j)
    ups(3)
    downs(3, 0, nd)
    for s in (2, 3):
        for j in (1, 2, 3, 0):
            @pl.loop(0, 4)
            def _(p):
                reduce1(s - 1, p, j).wait_recv()
                add(part, (s, rows(p, j), slice(None)), red1, (s - 2, rows(p, j), slice(None)))
                reduce1(s, p, j).start()
    for j in (1, 2, 3, 0):
        @pl.loop(0, 4)
        def _(p):
            reduce1(3, p, j).wait_recv()
            add(part, (0, rows(p, j), slice(None)), red1, (2, rows(p, j), slice(None)))
            if j != 1:
                k = 3 if j == 0 else j - 1
                reduce2(k, p).wait_recv()
                add(part, (0, rows(p, j), slice(None)), red2, (k - 1, rows(0, p), slice(None)))
            if j != 0:
                reduce2(j, p).start()
            else:
                out_ref[pl.ds(pl.multiple_of(p * ROWS, ROWS), ROWS), :] = part[0, rows(p, 0), :]

    @pl.loop(0, 4)
    def _(p):
        first_gather(0, p, 1, 0).wait_send()
        first_gather(1, p, 0, 1).wait_send()
        for j in (2, 3):
            gather(0, p, j).wait_send()
        for s in (1, 2, 3):
            for j in range(4):
                if s > 1 or j > 0:
                    gather(s, p, j).wait_send()
                reduce1(s, p, j).wait_send()
            reduce2(s, p).wait_send()


def plane_experts(arrived, up_local, down_local):
    slots, width = arrived.shape
    ffd = up_local.shape[1]
    bf = jnp.bfloat16
    dma = pltpu.SemaphoreType.DMA
    return pl.pallas_call(
        plane_kernel,
        out_shape=jax.ShapeDtypeStruct((slots, width), bf),
        in_specs=[
            pl.BlockSpec(memory_space=pltpu.VMEM),
            pl.BlockSpec(memory_space=pl.ANY),
            pl.BlockSpec(memory_space=pl.ANY),
        ],
        out_specs=pl.BlockSpec(memory_space=pltpu.VMEM),
        scratch_shapes=[
            pltpu.VMEM((4, 16 * ROWS, width), bf),
            pltpu.VMEM((4, 16 * ROWS, width), bf),
            pltpu.VMEM((3, 16 * ROWS, width), bf),
            pltpu.VMEM((3, 4 * ROWS, width), bf),
            pltpu.VMEM((16 * ROWS, ffd), bf),
            pltpu.VMEM((width, ffd), bf),
            pltpu.VMEM((ffd, width), bf),
            dma((2,)),
            dma((4, 4, 4)),
            dma((4, 4, 4)),
            dma((3, 4, 4)),
            dma((3, 4, 4)),
            dma((3, 4)),
            dma((3, 4)),
        ],
        compiler_params=pltpu.CompilerParams(
            collective_id=0, has_side_effects=True, vmem_limit_bytes=56 * 2**20
        ),
    )(arrived, up_local, down_local)


def body(
    residual,
    ssm_input,
    ssm_gate,
    input_map,
    output_map,
    step_raw,
    log_rate,
    skip_gain,
    head_gain,
    moe_gain,
    expert_ids,
    gate_weight,
    expert_up,
    expert_down,
):
    heads_loc = log_rate.shape[0]
    local_rows = residual.shape[1]
    width_loc = residual.shape[2]
    head_size = width_loc // heads_loc
    values = ssm_input[0].astype(jnp.float32).reshape(local_rows, heads_loc, head_size)
    step_size = jax.nn.softplus(step_raw[0])
    cumulative = jnp.cumsum(step_size * (-jnp.exp(log_rate))[None, :], axis=0)
    scores = jnp.einsum(
        "tn,sn->ts", output_map[0], input_map[0], preferred_element_type=jnp.float32
    )
    positions = jnp.arange(local_rows)
    causal = positions[:, None] >= positions[None, :]
    spread = cumulative[:, None, :] - cumulative[None, :, :]
    kernel = (
        jnp.where(causal[:, :, None], jnp.exp(jnp.minimum(spread, 0.0)), 0.0)
        * scores[:, :, None]
        * step_size[None, :, :]
    )
    within = jnp.einsum("tsh,shp->thp", kernel, values, precision=lax.Precision.HIGHEST)
    ending = cumulative[-1]
    carried = jnp.exp(ending[None, :] - cumulative) * step_size
    in_map_wide = input_map[0].astype(jnp.float32)
    out_map_wide = output_map[0].astype(jnp.float32)
    local_state = jnp.einsum(
        "sh,shp,sn->hpn", carried, values, in_map_wide, precision=lax.Precision.HIGHEST
    )
    total_decay = jnp.exp(ending)
    incoming = jnp.zeros_like(local_state)
    for repeat in range(lax.axis_size("ctx") - 1):
        outgoing = total_decay[:, None, None] * incoming + local_state
        incoming = shifted(outgoing.astype(jnp.bfloat16), "ctx", 1).astype(outgoing.dtype)
    across_heads = (
        jnp.einsum("tn,hpn->thp", out_map_wide, incoming, precision=lax.Precision.HIGHEST)
        * jnp.exp(cumulative)[:, :, None]
    )
    mixed_y = within + across_heads + skip_gain[None, :, None] * values
    gated = mixed_y * jax.nn.silu(
        ssm_gate[0].astype(jnp.float32).reshape(local_rows, heads_loc, head_size)
    )
    normed = (
        gated
        * lax.rsqrt(jnp.mean(gated * gated, axis=2, keepdims=True) + EPSILON)
        * head_gain.reshape(heads_loc, head_size)
    )
    hidden = (residual[0].astype(jnp.float32) + normed.reshape(local_rows, width_loc)).astype(
        jnp.bfloat16
    )
    exp_count = lax.axis_size("exp")
    my_expert = lax.axis_index("exp")
    tok_rows = local_rows // exp_count
    capacity = min(tok_rows, max(4, 4 * tok_rows // exp_count))
    model_width = width_loc * exp_count
    routes_all = expert_ids[0].reshape(exp_count, tok_rows, 2)
    slots_all = route_slots(routes_all, exp_count)
    targets_all = routes_all * capacity + slots_all
    slot_ids = jnp.arange(exp_count * capacity, dtype=jnp.int32)
    own_targets = lax.dynamic_slice_in_dim(targets_all, my_expert, 1, 0)[0]
    own_weights = lax.dynamic_slice_in_dim(
        gate_weight[0].reshape(exp_count, tok_rows, 2), my_expert, 1, 0
    )[0]
    tokens = lax.all_to_all(hidden, "exp", split_axis=0, concat_axis=1, tiled=True)
    tokens_wide = tokens.astype(jnp.float32)
    normal_rows = (
        tokens_wide
        * lax.rsqrt(jnp.mean(tokens_wide * tokens_wide, axis=1, keepdims=True) + EPSILON)
        * moe_gain[None, :]
    ).astype(jnp.bfloat16)
    placing = jnp.any(slot_ids[:, None, None] == own_targets[None, :, :], axis=2).astype(
        jnp.bfloat16
    )
    outbound = jnp.dot(placing, normal_rows, preferred_element_type=jnp.float32).astype(
        jnp.bfloat16
    )
    outbound = outbound.reshape(exp_count, capacity, model_width)
    arrived = lax.all_to_all(outbound, "exp", split_axis=0, concat_axis=0, tiled=True).reshape(
        exp_count * capacity, model_width
    )
    summed = plane_experts(arrived, expert_up[0], expert_down[0])
    sent_back = summed.reshape(exp_count, capacity, model_width)
    returned = lax.all_to_all(sent_back, "exp", split_axis=0, concat_axis=0, tiled=True).reshape(
        exp_count * capacity, model_width
    )
    picking = (own_targets.reshape(-1)[:, None] == slot_ids[None, :]).astype(jnp.bfloat16)
    chosen = jnp.dot(picking, returned, preferred_element_type=jnp.float32).reshape(
        tok_rows, 2, model_width
    )
    combined = jnp.sum(own_weights[:, :, None] * chosen, axis=1).astype(jnp.bfloat16)
    return (hidden[None], combined[None])


def solution(mesh):
    placed = (
        P("dp", "ctx", "exp"),
        P("dp", "ctx", "exp"),
        P("dp", "ctx", "exp"),
        P("dp", "ctx", None),
        P("dp", "ctx", None),
        P("dp", "ctx", "exp"),
        P("exp"),
        P("exp"),
        P("exp"),
        P(),
        P("dp", "ctx", None),
        P("dp", "ctx", None),
        P("exp", None, ("dp", "ctx")),
        P("exp", ("dp", "ctx"), None),
    )
    return jax.shard_map(
        body,
        mesh=mesh,
        in_specs=placed,
        out_specs=(P("dp", "ctx", "exp"), P("dp", ("ctx", "exp"), None)),
        check_vma=False,
    )
```
